256 devices in a mesh: tm: 8 (over z_hi, x), chan: 32 (over z_lo, y, core).
Axes of the slice: x: 4, y: 4, z: 8 (z_hi: 2, z_lo: 4; z = z_hi * 4 + z_lo), core: 2. Of those that a mesh axis runs over, the one named last changes fastest.
Arguments:
- voltage_frequency_samples: bfloat16 [2, 256, 30, 2, 8192], P(None, ('tm', 'chan')), may hold values from -6 to 6
- lag_lookup_entry: int32 [8, 8, 30], P('tm'), may hold values from 0 to 63
- lag_lookup_turning: float32 [64, 8192], P(None, 'chan'), may hold values from -3.140625 to 3.140625
- antenna_pair_members: int32 [435, 2], replicated, may hold values from 0 to 29, as said below
- frequency_bin_target: int32 [8192], P('chan'), may hold values from 0 to 63, as said below
Outputs:
- centre_vis: float32 [512, 2, 4, 435], P(('tm', 'chan'))
The draws below stay inside these ranges and needn't reach their ends.
Inputs may be any that keep to these rules, and one draw needn't show every extreme that they name: `antenna_pair_members`: every unordered pair of two different stations of the 30 appears in exactly one row, in either order. `frequency_bin_target`: each of the 64 output channels receives exactly 128 fine channels.
All inputs are finite; a program needn't handle non-finite values.
Results may differ from the reference program's by a relative error of at most 0.0029.
Values may be sent and summed in bfloat16 or wider, within the bound.
A program may use at most 128 MiB of HBM per device.

```python
import jax
import jax.numpy as jnp
import numpy as np
from jax import lax

S = 30
POL = 2
F = 8192
Q = 64
K = 64
C = 8
B = 435
SPECTRA = 256
SUBINTEGRATIONS = 8


def draw_antenna_pair_members(key, part):
    lower_np, upper_np = np.triu_indices(S, 1)
    station_pairs = jnp.stack([jnp.asarray(lower_np, jnp.int32), jnp.asarray(upper_np, jnp.int32)], axis=1)
    shuffle = jax.random.permutation(jax.random.fold_in(key, 11), B)
    station_pairs = station_pairs[shuffle]
    swapped = jax.random.randint(jax.random.fold_in(key, 12), (B,), 0, 2)
    return jnp.where(swapped[:, None] == 1, station_pairs[:, ::-1], station_pairs).astype(jnp.int32)


def draw_frequency_bin_target(key, part):
    shuffle = jax.random.permutation(jax.random.fold_in(key, 21), F)
    return (shuffle % Q).astype(jnp.int32)


def with_ends(result, own_key, least, top_value):
    extent = result.shape
    spot = [jax.random.randint(jax.random.fold_in(own_key, axis), (), 0, extent[axis]) for axis in range(len(extent))]
    result = result.at[tuple(spot)].set(least)
    longest = extent.index(max(extent))
    spot[longest] = (spot[longest] + 1) % extent[longest]
    return result.at[tuple(spot)].set(top_value)


def block_levels(own_key, shape, cuts, least, high):
    loudness = 1.0
    for dim, shards_of in cuts:
        heights = jax.random.uniform(jax.random.fold_in(jax.random.fold_in(own_key, 6), dim), (shards_of,), jnp.float32, least / len(cuts), high / len(cuts))
        loudness = loudness * jnp.repeat(jnp.exp(heights), shape[dim] // shards_of).reshape((-1,) + (1,) * (len(shape) - 1 - dim))
    return loudness


def scatter_about(stream_key, dims, width, bound, shards=(), held_as=jnp.bfloat16):
    array = jax.random.normal(stream_key, dims, jnp.float32) * width
    if len(shards) > 0:
        array = block_levels(stream_key, dims, shards, -0.22, 0.18) * array
    return jnp.clip(array, min=-bound, max=bound).astype(held_as)


def setup_inputs(seed: int = 0) -> dict:
    streams_of = jax.random.split(jax.random.key(seed), 6)
    return {
        "voltage_frequency_samples": scatter_about(streams_of[0], (2, SPECTRA, S, POL, F), 1.0, 6.0, ((1, 256),)),
        "lag_lookup_entry": with_ends(jax.random.randint(streams_of[1], (SUBINTEGRATIONS, C, S), 0, K), jax.random.fold_in(streams_of[1], 1), 0, K - 1).astype(jnp.int32),
        "lag_lookup_turning": jnp.clip(jax.random.uniform(streams_of[2], (K, F), jnp.float32, -3.140625, 3.140625), -3.140625, 3.140625),
        "antenna_pair_members": draw_antenna_pair_members(jax.random.fold_in(streams_of[5], 71), 0),
        "frequency_bin_target": draw_frequency_bin_target(jax.random.fold_in(streams_of[5], 71), 0),
    }


def reference(voltage_frequency_samples, lag_lookup_entry, lag_lookup_turning, antenna_pair_members, frequency_bin_target):
    per_group = SPECTRA // SUBINTEGRATIONS
    left_antenna_number = antenna_pair_members[:, 0]
    right_antenna_number = antenna_pair_members[:, 1]

    def correlate(left_part, right_part):
        return jnp.einsum("taf,tbf->abf", left_part.astype(jnp.float32), right_part.astype(jnp.float32))

    def one_group(carry, group):
        block = lax.dynamic_slice_in_dim(voltage_frequency_samples, (group * per_group).astype(jnp.int32), per_group, axis=1)
        real_part = block[0].reshape(per_group, S * POL, F)
        imag_part = block[1].reshape(per_group, S * POL, F)
        vis_real = correlate(real_part, real_part) + correlate(imag_part, imag_part)
        vis_imag = correlate(imag_part, real_part) - correlate(real_part, imag_part)
        vis_real = vis_real.reshape(S, POL, S, POL, F)[left_antenna_number, :, right_antenna_number].reshape(B, POL * POL, F)
        vis_imag = vis_imag.reshape(S, POL, S, POL, F)[left_antenna_number, :, right_antenna_number].reshape(B, POL * POL, F)
        phases = jnp.take(lag_lookup_turning, lag_lookup_entry[group], axis=0)
        phase_diff = phases[:, left_antenna_number] - phases[:, right_antenna_number]

        def rotate_one(angles):
            cosine = jnp.cos(angles)[:, None, :]
            sine = jnp.sin(angles)[:, None, :]
            rot_real = (vis_real * cosine + vis_imag * sine).astype(jnp.bfloat16)
            rot_imag = (vis_imag * cosine - vis_real * sine).astype(jnp.bfloat16)
            sum_real = jax.ops.segment_sum(jnp.moveaxis(rot_real.astype(jnp.float32), 2, 0), frequency_bin_target, num_segments=Q)
            sum_imag = jax.ops.segment_sum(jnp.moveaxis(rot_imag.astype(jnp.float32), 2, 0), frequency_bin_target, num_segments=Q)
            return jnp.stack([jnp.transpose(sum_real, (0, 2, 1)), jnp.transpose(sum_imag, (0, 2, 1))], axis=1)

        return carry + lax.map(rotate_one, phase_diff), None

    start = jnp.zeros((C, Q, 2, POL * POL, B), jnp.float32)
    total, _ = lax.scan(one_group, start, jnp.arange(SUBINTEGRATIONS, dtype=jnp.int32))
    return (total * (Q / F)).reshape(C * Q, 2, POL * POL, B)
```

```python
import functools

import jax
import jax.numpy as jnp
from jax import lax
from jax.experimental import pallas as pl
from jax.experimental.pallas import tpu as pltpu
from jax.sharding import PartitionSpec as P

F = 8192
Q = 64
S = 30
SP = 60
C = 8
K = 64
B = 435
OWN = 4096
STEP = 8192.0
MESH = pl.DeviceIdType.MESH
BF = jnp.bfloat16
F32 = jnp.float32


def place():
    tm = lax.axis_index("tm")
    ch = lax.axis_index("chan")
    return tm % 4, (ch // 2) % 4, (tm // 4) * 4 + ch // 8, ch % 2


def device(x, y, z, core):
    x, y, z = lax.rem(x + 4, 4), lax.rem(y + 4, 4), lax.rem(z + 8, 8)
    return ((z // 4) * 4 + x, (z % 4) * 8 + y * 2 + core)


def nt(a, b):
    return lax.dot_general(a, b, (((1,), (1,)), ((), ())), preferred_element_type=F32)


def gather_kernel(sh_ref, v_ref, full_ref, vp_ref, lsem, own_s, y_s, z_s, c_s, rsem, crsem, vsem):
    x, y, z, core = place()
    zl = z % 4
    partner = device(x, y, z, 1 - core)
    y_peers = [device(x, y + d, z, core) for d in (1, 2, 3)]
    z_peers = [device(x, y, z + d, core) for d in (1, 7, 2, 6)]
    barrier = pltpu.get_barrier_semaphore()
    for peer in [partner] + y_peers + z_peers:
        pl.semaphore_signal(barrier, inc=1, device_id=peer, device_id_type=MESH)
    pl.semaphore_wait(barrier, 8)

    vcopy = pltpu.make_async_remote_copy(
        src_ref=v_ref, dst_ref=vp_ref, send_sem=vsem.at[0], recv_sem=vsem.at[1],
        device_id=partner, device_id_type=MESH,
    )
    vcopy.start()

    def slot(zs, ys):
        return full_ref.at[core, zs, ys]

    def push(src, zs, ys, send, recv, peer):
        copy = pltpu.make_async_remote_copy(
            src_ref=src, dst_ref=slot(zs, ys), send_sem=send, recv_sem=recv,
            device_id=peer, device_id_type=MESH,
        )
        copy.start()
        return copy

    sent = []
    own = pltpu.make_async_copy(sh_ref, slot(zl, y), lsem)
    own.start()
    for n, peer in enumerate(y_peers):
        sent.append(push(sh_ref, zl, y, own_s.at[n], rsem.at[zl * 4 + y], peer))

    def spread(dy, src):
        ys = lax.rem(y + dy, 4)
        far = device(x, y, z + 2 + 4 * (ys % 2), core)
        for n, peer in enumerate([z_peers[0], z_peers[1], far]):
            sent.append(push(src, zl, ys, z_s.at[dy, n], rsem.at[zl * 4 + ys], peer))
        sent.append(push(src, zl, ys, c_s.at[0, dy], crsem.at[zl * 4 + ys], partner))

    def arrive(zs, ys):
        pltpu.make_async_remote_copy(
            src_ref=slot(zs, ys), dst_ref=slot(zs, ys), send_sem=lsem, recv_sem=rsem.at[zs * 4 + ys],
            device_id=partner, device_id_type=MESH,
        ).wait_recv()

    spread(0, sh_ref)
    for dy in (1, 3, 2):
        ys = lax.rem(y + dy, 4)
        arrive(zl, ys)
        spread(dy, slot(zl, ys))
    for dz in (1, 3, 2):
        zs = lax.rem(zl + dz, 4)
        for dy in (0, 1, 3, 2):
            ys = lax.rem(y + dy, 4)
            arrive(zs, ys)
            sent.append(push(slot(zs, ys), zs, ys, c_s.at[dz, dy], crsem.at[zs * 4 + ys], partner))
    for zs in range(4):
        for ys in range(4):
            other = full_ref.at[1 - core, zs, ys]
            pltpu.make_async_remote_copy(
                src_ref=other, dst_ref=other, send_sem=lsem, recv_sem=crsem.at[zs * 4 + ys],
                device_id=partner, device_id_type=MESH,
            ).wait_recv()
    for copy in sent:
        copy.wait_send()
    own.wait()
    vcopy.wait()


def gather(shard, volts):
    return pl.pallas_call(
        gather_kernel,
        out_shape=(
            jax.ShapeDtypeStruct((2, 4, 4) + shard.shape, shard.dtype),
            jax.ShapeDtypeStruct(volts.shape, volts.dtype),
        ),
        in_specs=[pl.BlockSpec(memory_space=pltpu.VMEM), pl.BlockSpec(memory_space=pl.ANY)],
        out_specs=(pl.BlockSpec(memory_space=pl.ANY), pl.BlockSpec(memory_space=pl.ANY)),
        scratch_shapes=[
            pltpu.SemaphoreType.DMA,
            pltpu.SemaphoreType.DMA((3,)),
            pltpu.SemaphoreType.DMA((1,)),
            pltpu.SemaphoreType.DMA((4, 3)),
            pltpu.SemaphoreType.DMA((4, 4)),
            pltpu.SemaphoreType.DMA((16,)),
            pltpu.SemaphoreType.DMA((16,)),
            pltpu.SemaphoreType.DMA((2,)),
        ],
        compiler_params=pltpu.CompilerParams(collective_id=0, has_side_effects=True),
        name="gather",
    )(shard, volts)


def sin_cos(phase):
    h = phase * 0.5
    u = h * h
    s = h * (1.0 + u * (-1.6666666666666666e-1 + u * (8.3333333333333332e-3 + u * (
        -1.9841269841269841e-4 + u * (2.7557319223985893e-6 + u * (-2.5052108385441720e-8 + u * 1.6059043836821613e-10))))))
    c = 1.0 + u * (-0.5 + u * (4.1666666666666664e-2 + u * (-1.3888888888888889e-3 + u * (
        2.4801587301587302e-5 + u * (-2.7557319223985888e-7 + u * (2.0876756987868100e-9 + u * -1.1470745597729725e-11))))))
    return 2.0 * s * c, 1.0 - 2.0 * s * s


def halves(value):
    hi = value.astype(BF)
    return hi, (value - hi.astype(F32)).astype(BF)


def local_kernel(va_ref, vb_ref, full_ref, pick_ref, ax_ref, by_ref, grid_ref, sorted_ref, perm_ref, perm_smem, cs_ref, sem):
    core = lax.axis_index("chan") % 2
    lane = lambda r, c: lax.broadcasted_iota(jnp.int32, (r, c), 1)
    row = lambda r, c: lax.broadcasted_iota(jnp.int32, (r, c), 0)

    kk = row(32, 1)
    bin_of = 4 * (kk // 2) + 2 * core + kk % 2
    before = (row(256, 256) < lane(256, 256)).astype(BF)
    fine = lane(1, 256).astype(F32)

    def rank_step(n, carry):
        base, high, low = carry
        target = full_ref[n % 2, n // 8, (n // 2) % 4, K : K + 1, :].astype(jnp.int32)
        member = bin_of == target
        ones = member.astype(F32)
        a = ones.astype(BF)
        ahead = jnp.dot(a, before, preferred_element_type=F32) + base
        rank = jnp.sum(ones * ahead, axis=0, keepdims=True).astype(jnp.int32)
        spot = (row(128, 256) == rank).astype(F32)
        where = jnp.concatenate([(spot * fine).astype(BF), spot.astype(BF)], axis=0)
        got = nt(a, where)
        low = low + got[:, :128]
        high = high + got[:, 128:] * n.astype(F32)
        return base + jnp.sum(ones, axis=1, keepdims=True), high, low

    zero = jnp.zeros((32, 128), F32)
    _, high, low = lax.fori_loop(0, 32, rank_step, (jnp.zeros((32, 1), F32), zero, zero), unroll=8)
    perm_ref[...] = (high * 256.0 + low).astype(jnp.int32)
    down = pltpu.make_async_copy(perm_ref, perm_smem, sem)
    down.start()

    eye = (row(256, 256) == lane(256, 256)).astype(BF)
    blank = jnp.zeros((8, 256), BF)

    def turn_step(n, _):
        at = pl.multiple_of(n * 256, 256)
        both = jnp.concatenate(
            [va_ref[:, :, pl.ds(at, 256)].reshape(120, 256), blank, vb_ref[:, :, pl.ds(at, 256)].reshape(120, 256), blank], axis=0
        )
        rows = nt(eye, both)
        grid_ref[pl.ds(at, 256), 0, :] = rows[:, :128]
        grid_ref[pl.ds(at, 256), 1, :] = rows[:, 128:]
        phase = full_ref[n % 2, n // 8, (n // 2) % 4, :K, :].astype(jnp.int32).astype(F32) * (1.0 / STEP)
        sine, cosine = sin_cos(phase)
        chi, clo = halves(cosine)
        shi, slo = halves(sine)
        rows = nt(eye, jnp.concatenate([chi, shi, clo, slo], axis=0))
        grid_ref[pl.ds(at, 256), 2, :] = rows[:, :128]
        grid_ref[pl.ds(at, 256), 3, :] = rows[:, 128:]
        return 0

    lax.fori_loop(0, 32, turn_step, 0, unroll=2)
    down.wait()

    def move_step(n, _):
        for u in range(16):
            sorted_ref[n * 16 + u] = grid_ref[perm_smem[n // 8, (n % 8) * 16 + u]]
        return 0

    lax.fori_loop(0, OWN // 16, move_step, 0)

    spread = row(128, 128)
    source = jnp.where(spread < 64, spread, spread - 4)
    fits = (spread % 64) < SP
    choose = ((source == lane(128, 128)) & fits).astype(BF)
    upper = row(64, 128) < lane(64, 128) % 64
    first = lane(64, 128) < 64

    def work_step(k, _):
        at = pl.multiple_of(k * 256, 256)
        va = nt(choose, sorted_ref[pl.ds(at, 256), 0, :].astype(BF))
        vb = nt(choose, sorted_ref[pl.ds(at, 256), 1, :].astype(BF))
        table = jnp.concatenate(
            [sorted_ref[pl.ds(at, 256), 2, :].astype(BF), sorted_ref[pl.ds(at, 256), 3, :].astype(BF)], axis=1
        )
        cs_ref[...] = nt(pick_ref[...], table)
        zl, y = k // 4, k % 4
        for c in range(C):
            cosine = cs_ref[c * 128 : c * 128 + 64, :]
            sine = cs_ref[c * 128 + 64 : c * 128 + 128, :]
            parts = []
            for v in (va, vb):
                re, im = v[:64], v[64:]
                turned = jnp.concatenate([re * cosine + im * sine, im * cosine - re * sine], axis=0)
                hi, lo = halves(turned)
                parts.append(jnp.concatenate([hi, lo], axis=0))
            got = []
            for r in range(2):
                w = jnp.concatenate([p[:, r * 128 : (r + 1) * 128] for p in parts], axis=1)
                zz = nt(w, w)
                zz = zz[:128, :128] + zz[:128, 128:] + zz[128:, :128]
                turn = pltpu.roll(zz[64:], 64, 1)
                got.append(zz[:64] + jnp.where(first, turn, -turn))
            d0, d1 = got
            e0, e1 = pltpu.roll(d0, 64, 1), pltpu.roll(d1, 64, 1)
            packed = jnp.where(upper, jnp.where(first, d0, e1), jnp.where(first, e0, d1)).astype(BF)
            xx, zz = c % 4, (c // 4) * 4 + zl
            ax_ref[xx, y, zz] = packed[:32]
            by_ref[y, xx, zz] = packed[32:]
        return 0

    lax.fori_loop(0, 16, work_step, 0)


def local_work(va, vb, full, pick):
    vm = pl.BlockSpec(memory_space=pltpu.VMEM)
    half = jax.ShapeDtypeStruct((4, 4, 8, 32, 128), BF)
    return pl.pallas_call(
        local_kernel,
        out_shape=(half, half),
        in_specs=[vm] * 4,
        out_specs=(vm, vm),
        scratch_shapes=[
            pltpu.VMEM((F, 4, 128), F32),
            pltpu.VMEM((OWN, 4, 128), F32),
            pltpu.VMEM((32, 128), jnp.int32),
            pltpu.SMEM((32, 128), jnp.int32),
            pltpu.VMEM((C * 128, 256), F32),
            pltpu.SemaphoreType.DMA,
        ],
        compiler_params=pltpu.CompilerParams(vmem_limit_bytes=66 * 1000 * 1000),
        name="local_work",
    )(va, vb, full, pick)


def sum_kernel(ax_ref, by_ref, out_ref, ra, rb, s1a, s1b, r2a, r2b, s2, r3, s1_s, s1_r, s2_s, s2_r, s3_s, s3_r):
    x, y, z, core = place()
    x_peers = [device(x + d, y, z, core) for d in (1, 2, 3)]
    y_peers = [device(x, y + d, z, core) for d in (1, 2, 3)]
    z_peers = [device(x, y, z + d, core) for d in range(1, 8)]
    barrier = pltpu.get_barrier_semaphore()
    for peer in x_peers + y_peers + z_peers:
        pl.semaphore_signal(barrier, inc=1, device_id=peer, device_id_type=MESH)
    pl.semaphore_wait(barrier, 13)

    def push(src, dst, send, recv, peer):
        copy = pltpu.make_async_remote_copy(
            src_ref=src, dst_ref=dst, send_sem=send, recv_sem=recv, device_id=peer, device_id_type=MESH
        )
        copy.start()
        return copy

    sides = (
        (0, ax_ref, ra, s1a, r2a, x, y, x_peers, y_peers),
        (1, by_ref, rb, s1b, r2b, y, x, y_peers, x_peers),
    )
    first = []
    for j in range(4):
        for h, src, dst, _, _, p, q, peers, _ in sides:
            part = lax.rem(q + 1 + j, 4)
            for d in range(3):
                to = lax.rem(p + d + 1, 4)
                first.append((h, j, d, push(
                    src.at[to, part], dst.at[d, part], s1_s.at[h, j, d], s1_r.at[h, j, d], peers[d])))
    index = {(h, j, d): copy for h, j, d, copy in first}
    second = []
    for j in range(4):
        for h, src, dst, held, land, p, q, _, peers in sides:
            part = lax.rem(q + 1 + j, 4)
            for d in range(3):
                index[h, j, d].wait_recv()
            total = src[p, part].astype(F32)
            for d in range(3):
                total = total + dst[d, part].astype(F32)
            held[j] = total
            if j < 3:
                second.append((h, j, push(
                    held.at[j], land.at[j], s2_s.at[h, j], s2_r.at[h, j], peers[j])))
    for h, _, _, held, land, *_ in sides:
        for hh, j, copy in second:
            if hh == h:
                copy.wait_recv()
        s2[:, h * 32 : h * 32 + 32, :] = held[3] + land[0] + land[1] + land[2]
    third = []
    for d in range(7):
        to = lax.rem(z + d + 1, 8)
        third.append(push(s2.at[to], r3.at[d], s3_s.at[d], s3_r.at[d], z_peers[d]))
    total = s2[z]
    for d in range(7):
        third[d].wait_recv()
        total = total + r3[d]
    out_ref[...] = total
    for copy in [c for *_, c in first] + [c for *_, c in second] + third:
        copy.wait_send()


def slice_sum(ax, by):
    vm = pl.BlockSpec(memory_space=pltpu.VMEM)
    return pl.pallas_call(
        sum_kernel,
        out_shape=jax.ShapeDtypeStruct((64, 128), F32),
        in_specs=[vm, vm],
        out_specs=vm,
        scratch_shapes=[
            pltpu.VMEM((3, 4, 8, 32, 128), BF),
            pltpu.VMEM((3, 4, 8, 32, 128), BF),
            pltpu.VMEM((4, 8, 32, 128), F32),
            pltpu.VMEM((4, 8, 32, 128), F32),
            pltpu.VMEM((3, 8, 32, 128), F32),
            pltpu.VMEM((3, 8, 32, 128), F32),
            pltpu.VMEM((8, 64, 128), F32),
            pltpu.VMEM((7, 64, 128), F32),
            pltpu.SemaphoreType.DMA((2, 4, 3)),
            pltpu.SemaphoreType.DMA((2, 4, 3)),
            pltpu.SemaphoreType.DMA((2, 3)),
            pltpu.SemaphoreType.DMA((2, 3)),
            pltpu.SemaphoreType.DMA((7,)),
            pltpu.SemaphoreType.DMA((7,)),
        ],
        compiler_params=pltpu.CompilerParams(
            collective_id=1, has_side_effects=True, vmem_limit_bytes=32 * 1000 * 1000
        ),
        name="slice_sum",
    )(ax, by)


def select_kernel(m_ref, pairs_ref, out_ref):
    one, two = pairs_ref[0:1, :], pairs_ref[1:2, :]
    least, most = jnp.minimum(one, two), jnp.maximum(one, two)
    sign = jnp.where(one < two, 1.0, -1.0).astype(F32)
    rows = lax.broadcasted_iota(jnp.int32, (64, 512), 0)
    columns = jnp.concatenate([(rows == 2 * most + p).astype(BF) for p in range(2)]
                              + [(rows == 2 * least + p).astype(BF) for p in range(2)], axis=1)
    m = m_ref[...] * (Q / F)
    m = jnp.concatenate([m[:, :64], m[:, 64:]], axis=0)
    m0 = m.astype(BF)
    rest = m - m0.astype(F32)
    m1 = rest.astype(BF)
    m2 = (rest - m1.astype(F32)).astype(BF)
    got = sum(jnp.dot(part, columns, preferred_element_type=F32) for part in (m0, m1, m2))
    ahead = one < two
    for r in range(2):
        def cell(side, p_row, p_col):
            block = got[r * 64 : r * 64 + 64, (side * 2 + p_col) * 512 : (side * 2 + p_col + 1) * 512]
            station = least if side == 0 else most
            return jnp.sum(jnp.where(rows == 2 * station + p_row, block, 0.0), axis=0, keepdims=True)
        upper = {(a, b): cell(0, a, b) for a in range(2) for b in range(2)}
        lower = {(a, b): cell(1, b, a) for a in range(2) for b in range(2)}
        for p in range(2):
            for p2 in range(2):
                re = jnp.where(ahead, upper[p, p2], upper[p2, p])
                im = sign * jnp.where(ahead, lower[p, p2], lower[p2, p])
                at = r * 8 + p * 2 + p2
                out_ref[at : at + 1, :] = re
                out_ref[at + 4 : at + 5, :] = im


def select(m, pairs):
    return pl.pallas_call(
        select_kernel,
        out_shape=jax.ShapeDtypeStruct((16, 512), F32),
        name="select",
    )(m, pairs)


def on_device(voltage_frequency_samples, lag_lookup_entry, lag_lookup_turning, antenna_pair_members, frequency_bin_target):
    volts = voltage_frequency_samples.reshape(SP, 2, F)
    fixed = jnp.round(lag_lookup_turning * STEP).astype(jnp.int16)
    target = jnp.broadcast_to(frequency_bin_target.astype(jnp.int16)[None, :], (16, F // 32))
    shard = jnp.concatenate([fixed, target], axis=0)

    entry = jnp.repeat(lag_lookup_entry[0], 2, axis=1)
    entry = jnp.pad(entry, ((0, 0), (0, 64 - SP)), constant_values=-1000)
    entry = jnp.stack([entry, entry + K], axis=1).reshape(C * 128, 1)
    pick = (entry == jnp.arange(256, dtype=jnp.int32)[None, :] % 128).astype(BF)

    pairs = jnp.pad(antenna_pair_members.T, ((0, 6), (0, 512 - B)))

    full, other = gather(shard, volts)
    ax, by = local_work(volts, other, full, pick)
    m = slice_sum(ax, by)
    return select(m, pairs)[:, :B].reshape(2, 2, 4, B)


def solution(mesh):
    return jax.shard_map(
        on_device,
        mesh=mesh,
        in_specs=(
            P(None, ("tm", "chan"), None, None, None),
            P("tm", None, None),
            P(None, "chan"),
            P(),
            P("chan"),
        ),
        out_specs=P(("tm", "chan"), None, None, None),
        check_vma=False,
    )
```

```python
import functools

import jax
import jax.numpy as jnp
from jax import lax
from jax.experimental import pallas as pl
from jax.experimental.pallas import tpu as pltpu
from jax.sharding import PartitionSpec as P

F = 8192
Q = 64
S = 30
SP = 60
C = 8
K = 64
B = 435
OWN = 4096
STEP = 8192.0
MESH = pl.DeviceIdType.MESH
BF = jnp.bfloat16
F32 = jnp.float32


def place():
    tm = lax.axis_index("tm")
    ch = lax.axis_index("chan")
    return tm % 4, (ch // 2) % 4, (tm // 4) * 4 + ch // 8, ch % 2


def device(x, y, z, core):
    x, y, z = lax.rem(x + 4, 4), lax.rem(y + 4, 4), lax.rem(z + 8, 8)
    return ((z // 4) * 4 + x, (z % 4) * 8 + y * 2 + core)


def nt(a, b):
    return lax.dot_general(a, b, (((1,), (1,)), ((), ())), preferred_element_type=F32)


def gather_kernel(sh_ref, v_ref, full_ref, vp_ref, lsem, own_s, y_s, z_s, c_s, rsem, crsem, vsem):
    x, y, z, core = place()
    zl = z % 4
    partner = device(x, y, z, 1 - core)
    y_peers = [device(x, y + d, z, core) for d in (1, 2, 3)]
    z_peers = [device(x, y, z + d, core) for d in (1, 7, 2, 6)]
    barrier = pltpu.get_barrier_semaphore()
    for peer in [partner] + y_peers + z_peers:
        pl.semaphore_signal(barrier, inc=1, device_id=peer, device_id_type=MESH)
    pl.semaphore_wait(barrier, 8)

    vcopy = pltpu.make_async_remote_copy(
        src_ref=v_ref, dst_ref=vp_ref, send_sem=vsem.at[0], recv_sem=vsem.at[1],
        device_id=partner, device_id_type=MESH,
    )
    vcopy.start()

    def slot(zs, ys):
        return full_ref.at[core, zs, ys]

    def push(src, zs, ys, send, recv, peer):
        copy = pltpu.make_async_remote_copy(
            src_ref=src, dst_ref=slot(zs, ys), send_sem=send, recv_sem=recv,
            device_id=peer, device_id_type=MESH,
        )
        copy.start()
        return copy

    sent = []
    own = pltpu.make_async_copy(sh_ref, slot(zl, y), lsem)
    own.start()
    for n, peer in enumerate(y_peers):
        sent.append(push(sh_ref, zl, y, own_s.at[n], rsem.at[zl * 4 + y], peer))

    def spread(dy, src):
        ys = lax.rem(y + dy, 4)
        far = device(x, y, z + 2 + 4 * (ys % 2), core)
        for n, peer in enumerate([z_peers[0], z_peers[1], far]):
            sent.append(push(src, zl, ys, z_s.at[dy, n], rsem.at[zl * 4 + ys], peer))
        sent.append(push(src, zl, ys, c_s.at[0, dy], crsem.at[zl * 4 + ys], partner))

    def arrive(zs, ys):
        pltpu.make_async_remote_copy(
            src_ref=slot(zs, ys), dst_ref=slot(zs, ys), send_sem=lsem, recv_sem=rsem.at[zs * 4 + ys],
            device_id=partner, device_id_type=MESH,
        ).wait_recv()

    spread(0, sh_ref)
    for dy in (1, 3, 2):
        ys = lax.rem(y + dy, 4)
        arrive(zl, ys)
        spread(dy, slot(zl, ys))
    for dz in (1, 3, 2):
        zs = lax.rem(zl + dz, 4)
        for dy in (0, 1, 3, 2):
            ys = lax.rem(y + dy, 4)
            arrive(zs, ys)
            sent.append(push(slot(zs, ys), zs, ys, c_s.at[dz, dy], crsem.at[zs * 4 + ys], partner))
    for zs in range(4):
        for ys in range(4):
            other = full_ref.at[1 - core, zs, ys]
            pltpu.make_async_remote_copy(
                src_ref=other, dst_ref=other, send_sem=lsem, recv_sem=crsem.at[zs * 4 + ys],
                device_id=partner, device_id_type=MESH,
            ).wait_recv()
    for copy in sent:
        copy.wait_send()
    own.wait()
    vcopy.wait()


def gather(shard, volts):
    return pl.pallas_call(
        gather_kernel,
        out_shape=(
            jax.ShapeDtypeStruct((2, 4, 4) + shard.shape, shard.dtype),
            jax.ShapeDtypeStruct(volts.shape, volts.dtype),
        ),
        in_specs=[pl.BlockSpec(memory_space=pltpu.VMEM), pl.BlockSpec(memory_space=pl.ANY)],
        out_specs=(pl.BlockSpec(memory_space=pl.ANY), pl.BlockSpec(memory_space=pl.ANY)),
        scratch_shapes=[
            pltpu.SemaphoreType.DMA,
            pltpu.SemaphoreType.DMA((3,)),
            pltpu.SemaphoreType.DMA((1,)),
            pltpu.SemaphoreType.DMA((4, 3)),
            pltpu.SemaphoreType.DMA((4, 4)),
            pltpu.SemaphoreType.DMA((16,)),
            pltpu.SemaphoreType.DMA((16,)),
            pltpu.SemaphoreType.DMA((2,)),
        ],
        compiler_params=pltpu.CompilerParams(collective_id=0, has_side_effects=True),
        name="gather",
    )(shard, volts)


def sin_cos(phase):
    h = phase * 0.5
    u = h * h
    s = h * (1.0 + u * (-1.6666666666666666e-1 + u * (8.3333333333333332e-3 + u * (
        -1.9841269841269841e-4 + u * (2.7557319223985893e-6 + u * (-2.5052108385441720e-8 + u * 1.6059043836821613e-10))))))
    c = 1.0 + u * (-0.5 + u * (4.1666666666666664e-2 + u * (-1.3888888888888889e-3 + u * (
        2.4801587301587302e-5 + u * (-2.7557319223985888e-7 + u * (2.0876756987868100e-9 + u * -1.1470745597729725e-11))))))
    return 2.0 * s * c, 1.0 - 2.0 * s * s


def halves(value):
    hi = value.astype(BF)
    return hi, (value - hi.astype(F32)).astype(BF)


def local_kernel(va_hbm, vb_hbm, full_ref, pick_ref, ax_ref, by_ref, grid_ref, s0_ref, s1_ref, perm_ref, perm_smem, cs_ref, va_ref, vb_ref, sem, load_sem):

    def load(part, side):
        here = (slice(None), slice(None), pl.ds(pl.multiple_of(part * 2048, 2048), 2048))
        src, dst = ((va_hbm, va_ref), (vb_hbm, vb_ref))[side]
        return pltpu.make_async_copy(src.at[here], dst.at[here], load_sem.at[side, part])

    for part in range(4):
        load(part, 0).start()
        load(part, 1).start()
    core = lax.axis_index("chan") % 2
    lane = lambda r, c: lax.broadcasted_iota(jnp.int32, (r, c), 1)
    row = lambda r, c: lax.broadcasted_iota(jnp.int32, (r, c), 0)

    kk = row(32, 1)
    bin_of = 4 * (kk // 2) + 2 * core + kk % 2
    before = (row(256, 256) < lane(256, 256)).astype(BF)
    fine = lane(1, 256).astype(F32)

    def rank_step(n, carry):
        base, high, low = carry
        target = full_ref[n % 2, n // 8, (n // 2) % 4, K : K + 1, :].astype(jnp.int32)
        member = bin_of == target
        ones = member.astype(F32)
        a = ones.astype(BF)
        ahead = jnp.dot(a, before, preferred_element_type=F32) + base
        rank = jnp.sum(ones * ahead, axis=0, keepdims=True).astype(jnp.int32)
        spot = (row(128, 256) == rank).astype(F32)
        where = jnp.concatenate([(spot * fine).astype(BF), spot.astype(BF)], axis=0)
        got = nt(a, where)
        low = low + got[:, :128]
        high = high + got[:, 128:] * n.astype(F32)
        return base + jnp.sum(ones, axis=1, keepdims=True), high, low

    zero = jnp.zeros((32, 128), F32)

    eye = (row(256, 256) == lane(256, 256)).astype(BF)
    blank = jnp.zeros((8, 256), BF)

    def turn_step(n, _):
        at = pl.multiple_of(n * 256, 256)
        both = jnp.concatenate(
            [va_ref[:, :, pl.ds(at, 256)].reshape(120, 256), blank, vb_ref[:, :, pl.ds(at, 256)].reshape(120, 256), blank], axis=0
        )
        rows = nt(eye, both)
        grid_ref[pl.ds(at, 256), 0, :] = rows[:, :128]
        grid_ref[pl.ds(at, 256), 1, :] = rows[:, 128:]
        phase = full_ref[n % 2, n // 8, (n // 2) % 4, :K, :].astype(jnp.int32).astype(F32) * (1.0 / STEP)
        sine, cosine = sin_cos(phase)
        chi, clo = halves(cosine)
        shi, slo = halves(sine)
        rows = nt(eye, jnp.concatenate([chi, shi, clo, slo], axis=0))
        grid_ref[pl.ds(at, 256), 2, :] = rows[:, :128]
        grid_ref[pl.ds(at, 256), 3, :] = rows[:, 128:]
        return 0

    def both_steps(n, carry):
        turn_step(n, 0)
        return rank_step(n, carry)

    def part_step(part, carry):
        load(part, 0).wait()
        load(part, 1).wait()
        return lax.fori_loop(0, 8, lambda n, held: both_steps(part * 8 + n, held), carry, unroll=8)

    _, high, low = lax.fori_loop(0, 4, part_step, (jnp.zeros((32, 1), F32), zero, zero))
    perm_ref[...] = (high * 256.0 + low).astype(jnp.int32)
    down = pltpu.make_async_copy(perm_ref, perm_smem, sem)
    down.start()
    down.wait()

    def move(dst, group, u):
        dst[u] = grid_ref[perm_smem[2 * group + u // 128, u % 128]]

    def move_step(n, _):
        for u in range(16):
            s0_ref[n * 16 + u] = grid_ref[perm_smem[n // 8, (n % 8) * 16 + u]]
        return 0

    lax.fori_loop(0, 16, move_step, 0)

    spread = row(128, 128)
    source = jnp.where(spread < 64, spread, spread - 4)
    fits = (spread % 64) < SP
    choose = ((source == lane(128, 128)) & fits).astype(BF)
    upper = row(64, 128) < lane(64, 128) % 64
    first = lane(64, 128) < 64

    def work(k, src, dst):
        ahead = jnp.minimum(k + 1, 15)
        va = nt(choose, src[:, 0, :].astype(BF))
        vb = nt(choose, src[:, 1, :].astype(BF))
        table = jnp.concatenate([src[:, 2, :].astype(BF), src[:, 3, :].astype(BF)], axis=1)
        cs_ref[...] = nt(pick_ref[...], table)
        zl, y = k // 4, k % 4
        for c in range(C):
            for u in range(32):
                move(dst, ahead, c * 32 + u)
            cosine = cs_ref[c * 128 : c * 128 + 64, :]
            sine = cs_ref[c * 128 + 64 : c * 128 + 128, :]
            parts = []
            for v in (va, vb):
                re, im = v[:64], v[64:]
                turned = jnp.concatenate([re * cosine + im * sine, im * cosine - re * sine], axis=0)
                hi, lo = halves(turned)
                parts.append(jnp.concatenate([hi, lo], axis=0))
            got = []
            for r in range(2):
                w = jnp.concatenate([p[:, r * 128 : (r + 1) * 128] for p in parts], axis=1)
                zz = nt(w, w)
                zz = zz[:128, :128] + zz[:128, 128:] + zz[128:, :128]
                turn = pltpu.roll(zz[64:], 64, 1)
                got.append(zz[:64] + jnp.where(first, turn, -turn))
            d0, d1 = got
            e0, e1 = pltpu.roll(d0, 64, 1), pltpu.roll(d1, 64, 1)
            packed = jnp.where(upper, jnp.where(first, d0, e1), jnp.where(first, e0, d1)).astype(BF)
            xx, zz = c % 4, (c // 4) * 4 + zl
            ax_ref[xx, y, zz] = packed[:32]
            by_ref[y, xx, zz] = packed[32:]

    def work_step(n, _):
        work(2 * n, s0_ref, s1_ref)
        work(2 * n + 1, s1_ref, s0_ref)
        return 0

    lax.fori_loop(0, 8, work_step, 0)


def local_work(va, vb, full, pick):
    vm = pl.BlockSpec(memory_space=pltpu.VMEM)
    hbm = pl.BlockSpec(memory_space=pl.ANY)
    half = jax.ShapeDtypeStruct((4, 4, 8, 32, 128), BF)
    return pl.pallas_call(
        local_kernel,
        out_shape=(half, half),
        in_specs=[hbm, hbm, vm, vm],
        out_specs=(vm, vm),
        scratch_shapes=[
            pltpu.VMEM((F, 4, 128), F32),
            pltpu.VMEM((256, 4, 128), F32),
            pltpu.VMEM((256, 4, 128), F32),
            pltpu.VMEM((32, 128), jnp.int32),
            pltpu.SMEM((32, 128), jnp.int32),
            pltpu.VMEM((C * 128, 256), F32),
            pltpu.VMEM((SP, 2, F), BF),
            pltpu.VMEM((SP, 2, F), BF),
            pltpu.SemaphoreType.DMA,
            pltpu.SemaphoreType.DMA((2, 4)),
        ],
        compiler_params=pltpu.CompilerParams(vmem_limit_bytes=66 * 1000 * 1000),
        name="local_work",
    )(va, vb, full, pick)


def sum_kernel(ax_ref, by_ref, out_ref, own_a, own_b, ra, rb, s1a, s1b, r2a, r2b, s2, r3, s1_s, s1_r, s2_s, s2_r, s3_s, s3_r, own_sem):
    x, y, z, core = place()
    mine = [
        pltpu.make_async_copy(ax_ref.at[x], own_a, own_sem.at[0]),
        pltpu.make_async_copy(by_ref.at[y], own_b, own_sem.at[1]),
    ]
    for copy in mine:
        copy.start()
    x_peers = [device(x + d, y, z, core) for d in (1, 2, 3)]
    y_peers = [device(x, y + d, z, core) for d in (1, 2, 3)]
    z_peers = [device(x, y, z + d, core) for d in range(1, 8)]
    barrier = pltpu.get_barrier_semaphore()
    for peer in x_peers + y_peers + z_peers:
        pl.semaphore_signal(barrier, inc=1, device_id=peer, device_id_type=MESH)
    pl.semaphore_wait(barrier, 13)

    def push(src, dst, send, recv, peer):
        copy = pltpu.make_async_remote_copy(
            src_ref=src, dst_ref=dst, send_sem=send, recv_sem=recv, device_id=peer, device_id_type=MESH
        )
        copy.start()
        return copy

    sides = (
        (0, ax_ref, ra, s1a, r2a, x, y, x_peers, y_peers),
        (1, by_ref, rb, s1b, r2b, y, x, y_peers, x_peers),
    )
    first = []
    for j in range(4):
        for h, src, dst, _, _, p, q, peers, _ in sides:
            part = lax.rem(q + 1 + j, 4)
            for d in range(3):
                to = lax.rem(p + d + 1, 4)
                first.append((h, j, d, push(
                    src.at[to, part], dst.at[d, part], s1_s.at[h, j, d], s1_r.at[h, j, d], peers[d])))
    index = {(h, j, d): copy for h, j, d, copy in first}
    for copy in mine:
        copy.wait()
    second = []
    for j in range(4):
        for h, src, dst, held, land, p, q, _, peers in sides:
            part = lax.rem(q + 1 + j, 4)
            for d in range(3):
                index[h, j, d].wait_recv()
            total = (own_a, own_b)[h][part].astype(F32)
            for d in range(3):
                total = total + dst[d, part].astype(F32)
            held[j] = total
            if j < 3:
                second.append((h, j, push(
                    held.at[j], land.at[j], s2_s.at[h, j], s2_r.at[h, j], peers[j])))
    for h, _, _, held, land, *_ in sides:
        for hh, j, copy in second:
            if hh == h:
                copy.wait_recv()
        s2[:, h * 32 : h * 32 + 32, :] = held[3] + land[0] + land[1] + land[2]
    third = []
    for d in range(7):
        to = lax.rem(z + d + 1, 8)
        third.append(push(s2.at[to], r3.at[d], s3_s.at[d], s3_r.at[d], z_peers[d]))
    total = s2[z]
    for d in range(7):
        third[d].wait_recv()
        total = total + r3[d]
    out_ref[...] = total
    for copy in [c for *_, c in first] + [c for *_, c in second] + third:
        copy.wait_send()


def slice_sum(ax, by):
    vm = pl.BlockSpec(memory_space=pltpu.VMEM)
    return pl.pallas_call(
        sum_kernel,
        out_shape=jax.ShapeDtypeStruct((64, 128), F32),
        in_specs=[pl.BlockSpec(memory_space=pl.ANY)] * 2,
        out_specs=vm,
        scratch_shapes=[
            pltpu.VMEM((4, 8, 32, 128), BF),
            pltpu.VMEM((4, 8, 32, 128), BF),
            pltpu.VMEM((3, 4, 8, 32, 128), BF),
            pltpu.VMEM((3, 4, 8, 32, 128), BF),
            pltpu.VMEM((4, 8, 32, 128), F32),
            pltpu.VMEM((4, 8, 32, 128), F32),
            pltpu.VMEM((3, 8, 32, 128), F32),
            pltpu.VMEM((3, 8, 32, 128), F32),
            pltpu.VMEM((8, 64, 128), F32),
            pltpu.VMEM((7, 64, 128), F32),
            pltpu.SemaphoreType.DMA((2, 4, 3)),
            pltpu.SemaphoreType.DMA((2, 4, 3)),
            pltpu.SemaphoreType.DMA((2, 3)),
            pltpu.SemaphoreType.DMA((2, 3)),
            pltpu.SemaphoreType.DMA((7,)),
            pltpu.SemaphoreType.DMA((7,)),
            pltpu.SemaphoreType.DMA((2,)),
        ],
        compiler_params=pltpu.CompilerParams(
            collective_id=1, has_side_effects=True, vmem_limit_bytes=32 * 1000 * 1000
        ),
        name="slice_sum",
    )(ax, by)


def select_kernel(m_ref, pairs_ref, out_ref):
    one, two = pairs_ref[0:1, :], pairs_ref[1:2, :]
    least, most = jnp.minimum(one, two), jnp.maximum(one, two)
    sign = jnp.where(one < two, 1.0, -1.0).astype(F32)
    rows = lax.broadcasted_iota(jnp.int32, (64, 512), 0)
    columns = jnp.concatenate([(rows == 2 * most + p).astype(BF) for p in range(2)]
                              + [(rows == 2 * least + p).astype(BF) for p in range(2)], axis=1)
    m = m_ref[...] * (Q / F)
    m = jnp.concatenate([m[:, :64], m[:, 64:]], axis=0)
    m0 = m.astype(BF)
    rest = m - m0.astype(F32)
    m1 = rest.astype(BF)
    m2 = (rest - m1.astype(F32)).astype(BF)
    got = sum(jnp.dot(part, columns, preferred_element_type=F32) for part in (m0, m1, m2))
    ahead = one < two
    for r in range(2):
        def cell(side, p_row, p_col):
            block = got[r * 64 : r * 64 + 64, (side * 2 + p_col) * 512 : (side * 2 + p_col + 1) * 512]
            station = least if side == 0 else most
            return jnp.sum(jnp.where(rows == 2 * station + p_row, block, 0.0), axis=0, keepdims=True)
        upper = {(a, b): cell(0, a, b) for a in range(2) for b in range(2)}
        lower = {(a, b): cell(1, b, a) for a in range(2) for b in range(2)}
        for p in range(2):
            for p2 in range(2):
                re = jnp.where(ahead, upper[p, p2], upper[p2, p])
                im = sign * jnp.where(ahead, lower[p, p2], lower[p2, p])
                at = r * 8 + p * 2 + p2
                out_ref[at : at + 1, :] = re
                out_ref[at + 4 : at + 5, :] = im


def select(m, pairs):
    return pl.pallas_call(
        select_kernel,
        out_shape=jax.ShapeDtypeStruct((16, 512), F32),
        name="select",
    )(m, pairs)


def on_device(voltage_frequency_samples, lag_lookup_entry, lag_lookup_turning, antenna_pair_members, frequency_bin_target):
    volts = voltage_frequency_samples.reshape(SP, 2, F)
    fixed = jnp.round(lag_lookup_turning * STEP).astype(jnp.int16)
    target = jnp.broadcast_to(frequency_bin_target.astype(jnp.int16)[None, :], (16, F // 32))
    shard = jnp.concatenate([fixed, target], axis=0)

    entry = jnp.repeat(lag_lookup_entry[0], 2, axis=1)
    entry = jnp.pad(entry, ((0, 0), (0, 64 - SP)), constant_values=-1000)
    entry = jnp.stack([entry, entry + K], axis=1).reshape(C * 128, 1)
    pick = (entry == jnp.arange(256, dtype=jnp.int32)[None, :] % 128).astype(BF)

    pairs = jnp.pad(antenna_pair_members.T, ((0, 6), (0, 512 - B)))

    full, other = gather(shard, volts)
    ax, by = local_work(volts, other, full, pick)
    m = slice_sum(ax, by)
    return select(m, pairs)[:, :B].reshape(2, 2, 4, B)


def solution(mesh):
    return jax.shard_map(
        on_device,
        mesh=mesh,
        in_specs=(
            P(None, ("tm", "chan"), None, None, None),
            P("tm", None, None),
            P(None, "chan"),
            P(),
            P("chan"),
        ),
        out_specs=P(("tm", "chan"), None, None, None),
        check_vma=False,
    )
```
